512 devices in a mesh: row: 32 (over y, z_lo), col: 16 (over z_hi, x, core).
Axes of the slice: x: 4, y: 8, z: 8 (z_hi: 2, z_lo: 4; z = z_hi * 4 + z_lo), core: 2. Of those that a mesh axis runs over, the one named last changes fastest.
Arguments:
- table: float32 [16, 256, 256], P('col', 'row'), may hold values from -4 to 4
- marginals: int32 [4096], replicated, may hold values from 64 to 4095
- visits: int32 [32, 16, 16], P('row', 'col'), may hold values from 0 to 15
- counts: int32 [32, 16, 16, 256, 256], P('row', 'col'), may hold values from 0 to 16, as said below
Outputs:
- gradient: float32 [16, 256, 256], P('col')
The draws below stay inside these ranges and needn't reach their ends.
Inputs may be any that keep to these rules, and one draw needn't show every extreme that they name: `counts`: about half of the cells of every tile are zero.
All inputs are finite; a program needn't handle non-finite values.
Results may differ from the reference program's by a relative error of at most 0.0031.
Values may be sent and summed in bfloat16 or wider, within the bound.
A program may use at most 128 MiB of HBM per device.

```python
import jax
import jax.numpy as jnp
from jax import lax

D = 256
B = 256
K = 16
NBLK = 16
VOCAB = 4096
N_ROW = 32
N_COL = 16


def draw_counts(key, part):
    shape_all = (N_ROW, N_COL, K, B, B)
    live_key, value_key = jax.random.split(jax.random.fold_in(key, 11))
    live = jax.random.randint(live_key, shape_all, 0, 2)
    values = jax.random.randint(value_key, shape_all, 1, 17)
    return jnp.where(live == 1, values, 0).astype(jnp.int32)


def with_ends(values, stream_key, smallest, top_value):
    index_at = [jax.random.randint(jax.random.fold_in(stream_key, axis), (), 0, length) for axis, length in enumerate(values.shape)]
    longest = values.shape.index(max(values.shape))
    beside = index_at[:longest] + [(index_at[longest] + 1) % values.shape[longest]] + index_at[longest + 1:]
    return values.at[tuple(index_at)].set(smallest).at[tuple(beside)].set(top_value)


def shard_levels(key, shape, pieces, smallest, top_value):
    factor_of, own = 1.0, jax.random.fold_in(key, 6)
    for dim, shards_of in pieces:
        draws = jnp.exp(jax.random.uniform(jax.random.fold_in(own, dim), (shards_of,), jnp.float32, smallest / len(pieces), top_value / len(pieces)))
        factor_of = factor_of * jnp.repeat(draws, shape[dim] // shards_of).reshape([-1 if axis == dim else 1 for axis in range(len(shape))])
    return factor_of


def bell_draw(key, extent, deviation, most, shards=(), held_as=jnp.bfloat16):
    loudness = shard_levels(key, extent, shards, -0.22, 0.18) if shards else 1.0
    entries = jax.random.normal(key, extent, jnp.float32) * deviation * loudness
    return jnp.minimum(jnp.maximum(entries, -most), most).astype(held_as)


def setup_inputs(seed: int = 0) -> dict:
    key_list = jax.random.split(jax.random.key(seed), 5)
    table = bell_draw(key_list[0], (NBLK, B, D), (D ** -0.25), 4.0, ((0, 16), (1, 32)), jnp.float32)
    marginals = with_ends(jax.random.randint(key_list[1], (VOCAB,), 64, 4096), jax.random.fold_in(key_list[1], 1), 64, 4095).astype(jnp.int32)
    visits = with_ends(jax.random.randint(key_list[2], (N_ROW, N_COL, K), 0, N_COL), jax.random.fold_in(key_list[2], 1), 0, N_COL - 1).astype(jnp.int32)
    counts = draw_counts(jax.random.fold_in(key_list[4], 71), 0)
    return {"table": table, "marginals": marginals, "visits": visits, "counts": counts}


LOSS_SCALE = 0.0625

def tile_terms(row_vectors, col_vectors, count_tile, log_rows, log_cols, log_total):
    logits = lax.dot_general(row_vectors, col_vectors, (((1,), (1,)), ((), ())), preferred_element_type=jnp.float32)
    count_vals = count_tile.astype(jnp.float32)
    baseline = log_total - log_rows[:, None] - log_cols[None, :]
    margin = logits - baseline
    fitted = (0.1 + 0.25 * jnp.sqrt(count_vals)) * (margin - jnp.log(jnp.maximum(count_vals, 1.0)))
    soft_hinge = jax.nn.sigmoid(margin)
    grad_logits = (jnp.where(count_vals > 0, fitted, soft_hinge) * LOSS_SCALE).astype(jnp.bfloat16)
    row_term = jnp.dot(grad_logits, col_vectors, preferred_element_type=jnp.float32)
    col_term = lax.dot_general(grad_logits, row_vectors, (((0,), (0,)), ((), ())), preferred_element_type=jnp.float32)
    return (row_term, col_term)

def reference(table, marginals, visits, counts):
    table_bf = table.astype(jnp.bfloat16)
    log_marg = jnp.log(marginals.astype(jnp.float32)).reshape(N_COL, B)
    log_total = jnp.log(jnp.sum(marginals).astype(jnp.float32))
    flat_visits = visits.reshape(N_ROW * N_COL, K)
    flat_counts = counts.reshape(N_ROW * N_COL, K, B, B)

    def device_step(running, scanned):
        device_id, visited, count_tiles = scanned
        own_block = device_id // N_COL % N_COL
        row_vectors = table_bf[own_block]
        log_rows = log_marg[own_block]
        partial_value = jnp.zeros((N_COL, B, D), jnp.float32)
        row_sum = jnp.zeros((B, D), jnp.float32)
        for k in range(K):
            visit_id = visited[k]
            row_term, col_term = tile_terms(row_vectors, table_bf[visit_id], count_tiles[k], log_rows, log_marg[visit_id], log_total)
            row_sum = row_sum + row_term
            partial_value = partial_value.at[visit_id].add(col_term)
        partial_value = partial_value.at[own_block].add(row_sum)
        return (running + partial_value, None)
    device_ids = jnp.arange(N_ROW * N_COL, dtype=jnp.int32)
    gradient, unused = lax.scan(device_step, jnp.zeros((N_COL, B, D), jnp.float32), (device_ids, flat_visits, flat_counts))
    return gradient
```

```python
import jax
import jax.numpy as jnp
from jax import lax
from jax.experimental import pallas as pl
from jax.experimental.pallas import tpu as pltpu
from jax.sharding import PartitionSpec as P

K = 16
MESH = pl.DeviceIdType.MESH
VMEM = pltpu.VMEM
F32 = jnp.float32
BF16 = jnp.bfloat16


def place():
    row = lax.axis_index("row")
    col = lax.axis_index("col")
    y, zl = lax.div(row, 4), lax.rem(row, 4)
    zh, x, core = lax.div(col, 8), lax.rem(lax.div(col, 2), 4), lax.rem(col, 2)
    return y, zl, zh, x, core


def device(y, zl, zh, x, core):
    return (y * 4 + zl, zh * 8 + x * 2 + core)


def partners(y, zl, zh, x, core):
    z = zh * 4 + zl
    found = [device(y, zl, zh, x, 1 - core)]
    for d in range(1, 4):
        found.append(device(y, zl, zh, lax.rem(x + d, 4), core))
    for d in range(1, 8):
        found.append(device(lax.rem(y + d, 8), zl, zh, x, core))
    for d in range(1, 8):
        other = lax.rem(z + d, 8)
        found.append(device(y, lax.rem(other, 4), lax.div(other, 4), x, core))
    return found


def greet(others):
    barrier = pltpu.get_barrier_semaphore()
    for other in others:
        pl.semaphore_signal(barrier, inc=1, device_id=other, device_id_type=MESH)
    pl.semaphore_wait(barrier, len(others))


def push(src, dst, send_sem, recv_sem, target):
    copy = pltpu.make_async_remote_copy(
        src_ref=src,
        dst_ref=dst,
        send_sem=send_sem,
        recv_sem=recv_sem,
        device_id=target,
        device_id_type=MESH,
    )
    copy.start()
    return copy


def arrive(dst, send_sem, recv_sem, target):
    pltpu.make_async_remote_copy(
        src_ref=dst,
        dst_ref=dst,
        send_sem=send_sem,
        recv_sem=recv_sem,
        device_id=target,
        device_id_type=MESH,
    ).wait_recv()


def gather_kernel(piece, full, zbuf, zs, zr, ys, yr, xs, xr, cs, cr):
    y, zl, zh, x, core = place()
    z = zh * 4 + zl
    greet(partners(y, zl, zh, x, core))
    mate = device(y, zl, zh, x, 1 - core)
    sent = []
    for d in (4, 3, 5, 2, 6, 1, 7):
        other = lax.rem(z + d, 8)
        target = device(y, lax.rem(other, 4), lax.div(other, 4), x, core)
        sent.append(push(piece, zbuf.at[z], zs.at[d], zr.at[d], target))
    zbuf[z] = piece[...]
    for d in range(1, 8):
        arrive(zbuf.at[lax.rem(z + 8 - d, 8)], zs.at[d], zr.at[d], mate)
    for h in range(2):
        full[h, x, core, y] = zbuf[h * 4 : h * 4 + 4].reshape(32, 256).astype(BF16)
    mine = full.at[:, x, core, y]
    for d in (4, 3, 5, 2, 6, 1, 7):
        target = device(lax.rem(y + d, 8), zl, zh, x, core)
        sent.append(push(mine, mine, ys.at[d], yr.at[d], target))
    order = (0, 1, 7, 2, 6, 3, 5, 4)
    for d in order:
        held = full.at[:, x, core, lax.rem(y + 8 - d, 8)]
        if d:
            arrive(held, ys.at[d], yr.at[d], mate)
        for e in (2, 1, 3):
            target = device(y, zl, zh, lax.rem(x + e, 4), core)
            sent.append(push(held, held, xs.at[d, e], xr.at[d, e], target))
        sent.append(push(held, held, cs.at[d, 0], cr.at[d, 0], mate))
    for d in order:
        for e in (1, 3, 2):
            held = full.at[:, lax.rem(x + 4 - e, 4), core, lax.rem(y + 8 - d, 8)]
            arrive(held, xs.at[d, e], xr.at[d, e], mate)
            sent.append(push(held, held, cs.at[d, e], cr.at[d, e], mate))
    for d in order:
        for e in range(4):
            held = full.at[:, lax.rem(x + 4 - e, 4), 1 - core, lax.rem(y + 8 - d, 8)]
            arrive(held, cs.at[d, e], cr.at[d, e], mate)
    for copy in sent:
        copy.wait_send()


def tile_kernel(visits, marg, table, counts, own_out, mate_out, log_marg, base, total):
    k = pl.program_id(0)
    own = lax.rem(lax.axis_index("row"), 16)
    core = lax.rem(lax.axis_index("col"), 2)

    @pl.when(k == 0)
    def _():
        log_marg[...] = jnp.log(marg[...].astype(F32))
        all_marg = marg[...]
        summed = jnp.sum(jnp.sum(all_marg, axis=0), axis=1, keepdims=True)
        log_total = jnp.log(summed.astype(F32))
        rows = jnp.broadcast_to(log_marg[own], (256, 256))
        base[...] = log_total - rows.T
        total[...] = jnp.zeros_like(total)

    visit = visits[k]
    row_vectors = table[own]
    col_vectors = table[visit]
    logits = lax.dot_general(
        row_vectors, col_vectors, (((1,), (1,)), ((), ())), preferred_element_type=F32
    )
    n = counts[0].astype(F32)
    margin = logits - (base[...] - log_marg[visit])
    m = jnp.maximum(n, 1.0)
    fitted = (0.1 + 0.25 * (m * lax.rsqrt(m))) * (margin - jnp.log(m))
    hinge = 0.5 * jnp.tanh(0.5 * margin) + 0.5
    g = (jnp.where(n > 0, fitted, hinge) * 0.0625).astype(BF16)
    total[own] += jnp.dot(g, col_vectors, preferred_element_type=F32)
    total[visit] += lax.dot_general(
        g, row_vectors, (((0,), (0,)), ((), ())), preferred_element_type=F32
    )

    @pl.when(k == K - 1)
    def _():
        for j in range(8):
            own_out[j] = total[2 * j + core]
            mate_out[j] = total[2 * j + 1 - core].astype(BF16)


def reduce_kernel(
    own, mate_part, out, cbuf, xout, xin, held, yout, yin, zout, zin,
    cs, cr, xs, xr, ys, yr, zs, zr, ls, lr, gs, gr,
):
    y, zl, zh, x, core = place()
    z = zh * 4 + zl
    greet(partners(y, zl, zh, x, core))
    mate = device(y, zl, zh, x, 1 - core)
    sent = []
    order = (4, 3, 5, 2, 6, 1, 7, 0)
    for d in order:
        q = lax.rem(y + d, 8)
        sent.append(push(mate_part.at[:, :, q], cbuf.at[:, :, q], cs.at[d], cr.at[d], mate))
    for d in order:
        q = lax.rem(y + d, 8)
        arrive(cbuf.at[:, :, q], cs.at[d], cr.at[d], mate)
        for e in (2, 1, 3):
            other = lax.rem(x + e, 4)
            xout[d, e] = (own[:, other, q] + cbuf[:, other, q].astype(F32)).astype(BF16)
            target = device(y, zl, zh, other, core)
            sent.append(push(xout.at[d, e], xin.at[d, e], xs.at[d, e], xr.at[d, e], target))
        held[d] = own[:, x, q] + cbuf[:, x, q].astype(F32)
    for d in order:
        for e in (1, 3, 2):
            arrive(xin.at[d, e], xs.at[d, e], xr.at[d, e], mate)
        part = (
            held[d] + xin[d, 1].astype(F32) + xin[d, 2].astype(F32) + xin[d, 3].astype(F32)
        )
        if d:
            yout[d] = part.astype(BF16)
            target = device(lax.rem(y + d, 8), zl, zh, x, core)
            sent.append(push(yout.at[d], yin.at[d], ys.at[d], yr.at[d], target))
        else:
            summed = part
    for d in (4, 3, 5, 2, 6, 1, 7):
        arrive(yin.at[d], ys.at[d], yr.at[d], mate)
        summed = summed + yin[d].astype(F32)
    zout[...] = summed.reshape(8, 8, 256)
    for d in (4, 3, 5, 2, 6, 1, 7):
        other = lax.rem(z + d, 8)
        target = device(y, lax.rem(other, 4), lax.div(other, 4), x, core)
        sent.append(push(zout.at[other], zin.at[d], zs.at[d], zr.at[d], target))
    last = zout[z]
    for d in (1, 7, 2, 6, 3, 5, 4):
        arrive(zin.at[d], zs.at[d], zr.at[d], mate)
        last = last + zin[d]
    out[y, zl] = last
    mine = out.at[y, zl]
    for e in (1, 2, 3):
        target = device(y, lax.rem(zl + e, 4), zh, x, core)
        sent.append(push(mine, mine, ls.at[e], lr.at[e], target))
    for e in range(4):
        piece = out.at[y, lax.rem(zl + 4 - e, 4)]
        if e:
            arrive(piece, ls.at[e], lr.at[e], mate)
        for d in (4, 3, 5, 2, 6, 1, 7):
            target = device(lax.rem(y + d, 8), zl, zh, x, core)
            sent.append(push(piece, piece, gs.at[e, d], gr.at[e, d], target))
    for e in range(4):
        for d in (1, 7, 2, 6, 3, 5, 4):
            piece = out.at[lax.rem(y + 8 - d, 8), lax.rem(zl + 4 - e, 4)]
            arrive(piece, gs.at[e, d], gr.at[e, d], mate)
    for copy in sent:
        copy.wait_send()


def whole():
    return pl.BlockSpec(memory_space=VMEM)


def local(table, marginals, visits, counts):
    sem = pltpu.SemaphoreType.DMA
    params = pltpu.CompilerParams
    full = pl.pallas_call(
        gather_kernel,
        out_shape=jax.ShapeDtypeStruct((2, 4, 2, 8, 32, 256), BF16),
        in_specs=[whole()],
        out_specs=whole(),
        scratch_shapes=[VMEM((8, 8, 256), F32)]
        + [sem((8,))] * 4
        + [sem((8, 4))] * 4,
        compiler_params=params(collective_id=0, has_side_effects=True),
        name="table_gather",
    )(table[0])
    full = full.reshape(16, 256, 256)
    own, mate_part = pl.pallas_call(
        tile_kernel,
        out_shape=[
            jax.ShapeDtypeStruct((8, 256, 256), F32),
            jax.ShapeDtypeStruct((8, 256, 256), BF16),
        ],
        grid_spec=pltpu.PrefetchScalarGridSpec(
            num_scalar_prefetch=1,
            grid=(K,),
            in_specs=[whole(), whole(), pl.BlockSpec((1, 256, 256), lambda k, v: (k, 0, 0))],
            out_specs=[whole(), whole()],
            scratch_shapes=[
                VMEM((16, 1, 256), F32),
                VMEM((256, 256), F32),
                VMEM((16, 256, 256), F32),
            ],
        ),
        name="tiles",
    )(visits[0, 0], marginals.reshape(16, 1, 256), full, counts[0, 0])
    out = pl.pallas_call(
        reduce_kernel,
        out_shape=jax.ShapeDtypeStruct((8, 4, 8, 256), F32),
        in_specs=[whole(), whole()],
        out_specs=whole(),
        scratch_shapes=[
            VMEM((2, 4, 8, 32, 256), BF16),
            VMEM((8, 4, 2, 32, 256), BF16),
            VMEM((8, 4, 2, 32, 256), BF16),
            VMEM((8, 2, 32, 256), F32),
            VMEM((8, 2, 32, 256), BF16),
            VMEM((8, 2, 32, 256), BF16),
            VMEM((8, 8, 256), F32),
            VMEM((8, 8, 256), F32),
            sem((8,)), sem((8,)),
            sem((8, 4)), sem((8, 4)),
            sem((8,)), sem((8,)),
            sem((8,)), sem((8,)),
            sem((4,)), sem((4,)),
            sem((4, 8)), sem((4, 8)),
        ],
        compiler_params=params(collective_id=1, has_side_effects=True),
        name="gradient_reduce",
    )(own.reshape(2, 4, 8, 32, 256), mate_part.reshape(2, 4, 8, 32, 256))
    return out.reshape(1, 256, 256)


def solution(mesh):
    return jax.shard_map(
        local,
        mesh=mesh,
        in_specs=(
            P("col", "row", None),
            P(),
            P("row", "col", None),
            P("row", "col", None, None, None),
        ),
        out_specs=P("col", None, None),
        check_vma=False,
    )
```

```python
import jax
import jax.numpy as jnp
from jax import lax
from jax.experimental import pallas as pl
from jax.experimental.pallas import tpu as pltpu
from jax.sharding import PartitionSpec as P

K = 16
MESH = pl.DeviceIdType.MESH
VMEM = pltpu.VMEM
F32 = jnp.float32
BF16 = jnp.bfloat16


def place():
    row = lax.axis_index("row")
    col = lax.axis_index("col")
    y, zl = lax.div(row, 4), lax.rem(row, 4)
    zh, x, core = lax.div(col, 8), lax.rem(lax.div(col, 2), 4), lax.rem(col, 2)
    return y, zl, zh, x, core


def device(y, zl, zh, x, core):
    return (y * 4 + zl, zh * 8 + x * 2 + core)


def partners(y, zl, zh, x, core):
    z = zh * 4 + zl
    found = [device(y, zl, zh, x, 1 - core)]
    for d in range(1, 4):
        found.append(device(y, zl, zh, lax.rem(x + d, 4), core))
    for d in range(1, 8):
        found.append(device(lax.rem(y + d, 8), zl, zh, x, core))
    for d in range(1, 8):
        other = lax.rem(z + d, 8)
        found.append(device(y, lax.rem(other, 4), lax.div(other, 4), x, core))
    return found


def greet(others):
    barrier = pltpu.get_barrier_semaphore()
    for other in others:
        pl.semaphore_signal(barrier, inc=1, device_id=other, device_id_type=MESH)
    pl.semaphore_wait(barrier, len(others))


def push(src, dst, send_sem, recv_sem, target):
    copy = pltpu.make_async_remote_copy(
        src_ref=src,
        dst_ref=dst,
        send_sem=send_sem,
        recv_sem=recv_sem,
        device_id=target,
        device_id_type=MESH,
    )
    copy.start()
    return copy


def arrive(dst, send_sem, recv_sem, target):
    pltpu.make_async_remote_copy(
        src_ref=dst,
        dst_ref=dst,
        send_sem=send_sem,
        recv_sem=recv_sem,
        device_id=target,
        device_id_type=MESH,
    ).wait_recv()


def gather_kernel(piece, full, zbuf, zs, zr, ys, yr, xs, xr, cs, cr):
    y, zl, zh, x, core = place()
    z = zh * 4 + zl
    greet(partners(y, zl, zh, x, core))
    mate = device(y, zl, zh, x, 1 - core)
    sent = []
    for d in (4, 3, 5, 2, 6, 1, 7):
        other = lax.rem(z + d, 8)
        target = device(y, lax.rem(other, 4), lax.div(other, 4), x, core)
        sent.append(push(piece, zbuf.at[z], zs.at[d], zr.at[d], target))
    zbuf[z] = piece[...]
    for d in range(1, 8):
        arrive(zbuf.at[lax.rem(z + 8 - d, 8)], zs.at[d], zr.at[d], mate)
    for h in range(2):
        full[h, x, core, y] = zbuf[h * 4 : h * 4 + 4].reshape(32, 256).astype(BF16)
    mine = full.at[:, x, core, y]
    for d in (4, 3, 5, 2, 6, 1, 7):
        target = device(lax.rem(y + d, 8), zl, zh, x, core)
        sent.append(push(mine, mine, ys.at[d], yr.at[d], target))
    right = device(y, zl, zh, lax.rem(x + 1, 4), core)
    left = device(y, zl, zh, lax.rem(x + 3, 4), core)
    order = (0, 1, 7, 2, 6, 3, 5, 4)

    def near(d):
        from_y = lax.rem(y + 8 - d, 8)
        held = full.at[:, x, core, from_y]
        if d:
            arrive(held, ys.at[d], yr.at[d], mate)
        sent.append(push(held, held, xs.at[d, 0], xr.at[d, 0], right))
        sent.append(push(held, held, xs.at[d, 1], xr.at[d, 1], left))
        sent.append(push(held, held, cs.at[d, 0], cr.at[d, 0], mate))

    def far(d):
        from_y = lax.rem(y + 8 - d, 8)
        before = full.at[:, lax.rem(x + 3, 4), core, from_y]
        after = full.at[:, lax.rem(x + 1, 4), core, from_y]
        arrive(before, xs.at[d, 0], xr.at[d, 0], mate)
        half = full.at[0, lax.rem(x + 3, 4), core, from_y]
        sent.append(push(half, half, xs.at[d, 2], xr.at[d, 2], right))
        arrive(after, xs.at[d, 1], xr.at[d, 1], mate)
        half = full.at[1, lax.rem(x + 1, 4), core, from_y]
        sent.append(push(half, half, xs.at[d, 3], xr.at[d, 3], left))
        sent.append(push(before, before, cs.at[d, 1], cr.at[d, 1], mate))
        sent.append(push(after, after, cs.at[d, 2], cr.at[d, 2], mate))

    def opposite(d):
        from_y = lax.rem(y + 8 - d, 8)
        for h in range(2):
            held = full.at[h, lax.rem(x + 2, 4), core, from_y]
            arrive(held, xs.at[d, 2 + h], xr.at[d, 2 + h], mate)
            sent.append(push(held, held, cs.at[d, 3 + h], cr.at[d, 3 + h], mate))

    for step in range(12):
        if step < 8:
            near(order[step])
        if 2 <= step < 10:
            far(order[step - 2])
        if step >= 4:
            opposite(order[step - 4])
    for d in order:
        from_y = lax.rem(y + 8 - d, 8)
        for e, source in ((0, x), (1, lax.rem(x + 3, 4)), (2, lax.rem(x + 1, 4))):
            held = full.at[:, source, 1 - core, from_y]
            arrive(held, cs.at[d, e], cr.at[d, e], mate)
        for h in range(2):
            held = full.at[h, lax.rem(x + 2, 4), 1 - core, from_y]
            arrive(held, cs.at[d, 3 + h], cr.at[d, 3 + h], mate)
    for copy in sent:
        copy.wait_send()


def tile_kernel(visits, marg, table, counts, own_out, mate_out, log_marg, base, total):
    k = pl.program_id(0)
    own = lax.rem(lax.axis_index("row"), 16)
    core = lax.rem(lax.axis_index("col"), 2)

    @pl.when(k == 0)
    def _():
        log_marg[...] = jnp.log(marg[...].astype(F32))
        all_marg = marg[...]
        summed = jnp.sum(jnp.sum(all_marg, axis=0), axis=1, keepdims=True)
        log_total = jnp.log(summed.astype(F32))
        rows = jnp.broadcast_to(log_marg[own], (256, 256))
        base[...] = log_total - rows.T
        total[...] = jnp.zeros_like(total)

    visit = visits[k]
    row_vectors = table[own]
    col_vectors = table[visit]
    logits = lax.dot_general(
        row_vectors, col_vectors, (((1,), (1,)), ((), ())), preferred_element_type=F32
    )
    n = counts[0].astype(F32)
    margin = logits - (base[...] - log_marg[visit])
    m = jnp.maximum(n, 1.0)
    fitted = (0.1 + 0.25 * (m * lax.rsqrt(m))) * (margin - jnp.log(m))
    hinge = 0.5 * jnp.tanh(0.5 * margin) + 0.5
    g = (jnp.where(n > 0, fitted, hinge) * 0.0625).astype(BF16)
    total[own] += jnp.dot(g, col_vectors, preferred_element_type=F32)
    total[visit] += lax.dot_general(
        g, row_vectors, (((0,), (0,)), ((), ())), preferred_element_type=F32
    )

    @pl.when(k == K - 1)
    def _():
        for j in range(8):
            own_out[j] = total[2 * j + core]
            mate_out[j] = total[2 * j + 1 - core].astype(BF16)


def reduce_kernel(
    own, mate_part, out, cbuf, xout, xin, kept, held, yout, yin, zout, zin,
    cs, cr, xs, xr, ys, yr, zs, zr, gs, gr,
):
    y, zl, zh, x, core = place()
    z = zh * 4 + zl
    greet(partners(y, zl, zh, x, core))
    mate = device(y, zl, zh, x, 1 - core)
    right_x, left_x, far_x = lax.rem(x + 1, 4), lax.rem(x + 3, 4), lax.rem(x + 2, 4)
    right = device(y, zl, zh, right_x, core)
    left = device(y, zl, zh, left_x, core)
    sent = []
    order = (4, 3, 5, 2, 6, 1, 7, 0)
    for d in order:
        q = lax.rem(y + d, 8)
        sent.append(push(mate_part.at[:, :, q], cbuf.at[:, :, q], cs.at[d], cr.at[d], mate))

    def send_x(d, slot, value, target):
        xout[d, slot] = value.astype(BF16)
        sent.append(push(xout.at[d, slot], xin.at[d, slot], xs.at[d, slot], xr.at[d, slot], target))

    def wait_x(d, slot):
        arrive(xin.at[d, slot], xs.at[d, slot], xr.at[d, slot], mate)
        return xin[d, slot].astype(F32)

    def first(d):
        q = lax.rem(y + d, 8)
        arrive(cbuf.at[:, :, q], cs.at[d], cr.at[d], mate)

        def chip(h, block):
            return own[h, block, q] + cbuf[h, block, q].astype(F32)

        send_x(d, 0, chip(0, far_x), right)
        send_x(d, 1, chip(1, far_x), left)
        send_x(d, 2, chip(1, right_x), right)
        send_x(d, 3, chip(0, left_x), left)
        kept[d, 0] = chip(0, right_x)
        kept[d, 1] = chip(1, left_x)
        held[d, 0] = chip(0, x)
        held[d, 1] = chip(1, x)

    def second(d):
        send_x(d, 4, kept[d, 0] + wait_x(d, 0), right)
        send_x(d, 5, kept[d, 1] + wait_x(d, 1), left)

    def third(d):
        low = held[d, 0] + wait_x(d, 3) + wait_x(d, 4)
        high = held[d, 1] + wait_x(d, 2) + wait_x(d, 5)
        if d:
            yout[d, 0] = low.astype(BF16)
            yout[d, 1] = high.astype(BF16)
            target = device(lax.rem(y + d, 8), zl, zh, x, core)
            sent.append(push(yout.at[d], yin.at[d], ys.at[d], yr.at[d], target))
        else:
            held[d, 0] = low
            held[d, 1] = high

    for step in range(12):
        if step < 8:
            first(order[step])
        if 2 <= step < 10:
            second(order[step - 2])
        if step >= 4:
            third(order[step - 4])
    summed = held[0]
    for d in (4, 3, 5, 2, 6, 1, 7):
        arrive(yin.at[d], ys.at[d], yr.at[d], mate)
        summed = summed + yin[d].astype(F32)
    zout[...] = summed.astype(BF16)
    for d in (4, 3, 5, 2, 6, 1, 7):
        other = lax.rem(z + d, 8)
        other_h = lax.div(other, 4)
        target = device(y, lax.rem(other, 4), other_h, x, core)
        sent.append(push(zout.at[other_h], zin.at[z], zs.at[d], zr.at[d], target))
    zin[z] = zout[zh]
    for d in (1, 7, 2, 6, 3, 5, 4):
        arrive(zin.at[lax.rem(z + 8 - d, 8)], zs.at[d], zr.at[d], mate)
    last = zin[0].astype(F32)
    for source in range(1, 8):
        last = last + zin[source].astype(F32)
    out[y] = last.astype(BF16)
    mine = out.at[y]
    for d in (4, 3, 5, 2, 6, 1, 7):
        target = device(lax.rem(y + d, 8), zl, zh, x, core)
        sent.append(push(mine, mine, gs.at[d], gr.at[d], target))
    for d in (1, 7, 2, 6, 3, 5, 4):
        arrive(out.at[lax.rem(y + 8 - d, 8)], gs.at[d], gr.at[d], mate)
    for copy in sent:
        copy.wait_send()


def whole():
    return pl.BlockSpec(memory_space=VMEM)


def local(table, marginals, visits, counts):
    sem = pltpu.SemaphoreType.DMA
    params = pltpu.CompilerParams
    full = pl.pallas_call(
        gather_kernel,
        out_shape=jax.ShapeDtypeStruct((2, 4, 2, 8, 32, 256), BF16),
        in_specs=[whole()],
        out_specs=whole(),
        scratch_shapes=[VMEM((8, 8, 256), F32)]
        + [sem((8,))] * 4
        + [sem((8, 4))] * 2
        + [sem((8, 5))] * 2,
        compiler_params=params(collective_id=0, has_side_effects=True),
        name="table_gather",
    )(table[0])
    full = full.reshape(16, 256, 256)
    own, mate_part = pl.pallas_call(
        tile_kernel,
        out_shape=[
            jax.ShapeDtypeStruct((8, 256, 256), F32),
            jax.ShapeDtypeStruct((8, 256, 256), BF16),
        ],
        grid_spec=pltpu.PrefetchScalarGridSpec(
            num_scalar_prefetch=1,
            grid=(K,),
            in_specs=[whole(), whole(), pl.BlockSpec((1, 256, 256), lambda k, v: (k, 0, 0))],
            out_specs=[whole(), whole()],
            scratch_shapes=[
                VMEM((16, 1, 256), F32),
                VMEM((256, 256), F32),
                VMEM((16, 256, 256), F32),
            ],
        ),
        name="tiles",
    )(visits[0, 0], marginals.reshape(16, 1, 256), full, counts[0, 0])
    out = pl.pallas_call(
        reduce_kernel,
        out_shape=jax.ShapeDtypeStruct((8, 32, 256), BF16),
        in_specs=[whole(), whole()],
        out_specs=whole(),
        scratch_shapes=[
            VMEM((2, 4, 8, 32, 256), BF16),
            VMEM((8, 6, 32, 256), BF16),
            VMEM((8, 6, 32, 256), BF16),
            VMEM((8, 2, 32, 256), F32),
            VMEM((8, 2, 32, 256), F32),
            VMEM((8, 2, 32, 256), BF16),
            VMEM((8, 2, 32, 256), BF16),
            VMEM((2, 32, 256), BF16),
            VMEM((8, 32, 256), BF16),
            sem((8,)), sem((8,)),
            sem((8, 6)), sem((8, 6)),
            sem((8,)), sem((8,)),
            sem((8,)), sem((8,)),
            sem((8,)), sem((8,)),
        ],
        compiler_params=params(collective_id=1, has_side_effects=True),
        name="gradient_reduce",
    )(own.reshape(2, 4, 8, 32, 256), mate_part.reshape(2, 4, 8, 32, 256))
    return out.reshape(1, 256, 256).astype(F32)


def solution(mesh):
    return jax.shard_map(
        local,
        mesh=mesh,
        in_specs=(
            P("col", "row", None),
            P(),
            P("row", "col", None),
            P("row", "col", None, None, None),
        ),
        out_specs=P("col", None, None),
        check_vma=False,
    )
```

```python
import jax
import jax.numpy as jnp
from jax import lax
from jax.experimental import pallas as pl
from jax.experimental.pallas import tpu as pltpu
from jax.sharding import PartitionSpec as P

K = 16
STEP = 2
MESH = pl.DeviceIdType.MESH
VMEM = pltpu.VMEM
F32 = jnp.float32
BF16 = jnp.bfloat16


def place():
    row = lax.axis_index("row")
    col = lax.axis_index("col")
    y, zl = lax.div(row, 4), lax.rem(row, 4)
    zh, x, core = lax.div(col, 8), lax.rem(lax.div(col, 2), 4), lax.rem(col, 2)
    return y, zl, zh, x, core


def device(y, zl, zh, x, core):
    return (y * 4 + zl, zh * 8 + x * 2 + core)


def partners(y, zl, zh, x, core):
    z = zh * 4 + zl
    found = [device(y, zl, zh, x, 1 - core)]
    for d in range(1, 4):
        found.append(device(y, zl, zh, lax.rem(x + d, 4), core))
    for d in range(1, 8):
        found.append(device(lax.rem(y + d, 8), zl, zh, x, core))
    for d in range(1, 8):
        other = lax.rem(z + d, 8)
        found.append(device(y, lax.rem(other, 4), lax.div(other, 4), x, core))
    return found


def greet(others):
    barrier = pltpu.get_barrier_semaphore()
    for other in others:
        pl.semaphore_signal(barrier, inc=1, device_id=other, device_id_type=MESH)
    pl.semaphore_wait(barrier, len(others))


def push(src, dst, send_sem, recv_sem, target):
    copy = pltpu.make_async_remote_copy(
        src_ref=src,
        dst_ref=dst,
        send_sem=send_sem,
        recv_sem=recv_sem,
        device_id=target,
        device_id_type=MESH,
    )
    copy.start()
    return copy


def arrive(dst, send_sem, recv_sem, target):
    pltpu.make_async_remote_copy(
        src_ref=dst,
        dst_ref=dst,
        send_sem=send_sem,
        recv_sem=recv_sem,
        device_id=target,
        device_id_type=MESH,
    ).wait_recv()


def gather_kernel(piece, full, zbuf, zs, zr, ys, yr, xs, xr, cs, cr):
    y, zl, zh, x, core = place()
    z = zh * 4 + zl
    greet(partners(y, zl, zh, x, core))
    mate = device(y, zl, zh, x, 1 - core)
    sent = []
    for d in (4, 3, 5, 2, 6, 1, 7):
        other = lax.rem(z + d, 8)
        target = device(y, lax.rem(other, 4), lax.div(other, 4), x, core)
        sent.append(push(piece, zbuf.at[z], zs.at[d], zr.at[d], target))
    zbuf[z] = piece[...]
    for d in range(1, 8):
        arrive(zbuf.at[lax.rem(z + 8 - d, 8)], zs.at[d], zr.at[d], mate)
    for h in range(2):
        full[h, x, core, y] = zbuf[h * 4 : h * 4 + 4].reshape(32, 256).astype(BF16)
    mine = full.at[:, x, core, y]
    up = device(lax.rem(y + 1, 8), zl, zh, x, core)
    down = device(lax.rem(y + 7, 8), zl, zh, x, core)
    sent.append(push(mine, mine, ys.at[0, 1], yr.at[0, 1], up))
    sent.append(push(mine, mine, ys.at[1, 1], yr.at[1, 1], down))
    right = device(y, zl, zh, lax.rem(x + 1, 4), core)
    left = device(y, zl, zh, lax.rem(x + 3, 4), core)
    order = (0, 1, 7, 2, 6, 3, 5, 4)

    def near(d):
        from_y = lax.rem(y + 8 - d, 8)
        held = full.at[:, x, core, from_y]
        if d == 4:
            arrive(full.at[0, x, core, from_y], ys.at[0, 4], yr.at[0, 4], mate)
            arrive(full.at[1, x, core, from_y], ys.at[1, 4], yr.at[1, 4], mate)
        elif d:
            side, hops = (0, d) if d < 4 else (1, 8 - d)
            arrive(held, ys.at[side, hops], yr.at[side, hops], mate)
            part = held if hops < 3 else full.at[side, x, core, from_y]
            send_sem, recv_sem = ys.at[side, hops + 1], yr.at[side, hops + 1]
            sent.append(push(part, part, send_sem, recv_sem, (up, down)[side]))
        sent.append(push(held, held, xs.at[d, 0], xr.at[d, 0], right))
        sent.append(push(held, held, xs.at[d, 1], xr.at[d, 1], left))
        sent.append(push(held, held, cs.at[d, 0], cr.at[d, 0], mate))

    def far(d):
        from_y = lax.rem(y + 8 - d, 8)
        before = full.at[:, lax.rem(x + 3, 4), core, from_y]
        after = full.at[:, lax.rem(x + 1, 4), core, from_y]
        arrive(before, xs.at[d, 0], xr.at[d, 0], mate)
        half = full.at[0, lax.rem(x + 3, 4), core, from_y]
        sent.append(push(half, half, xs.at[d, 2], xr.at[d, 2], right))
        arrive(after, xs.at[d, 1], xr.at[d, 1], mate)
        half = full.at[1, lax.rem(x + 1, 4), core, from_y]
        sent.append(push(half, half, xs.at[d, 3], xr.at[d, 3], left))
        sent.append(push(before, before, cs.at[d, 1], cr.at[d, 1], mate))
        sent.append(push(after, after, cs.at[d, 2], cr.at[d, 2], mate))

    def opposite(d):
        from_y = lax.rem(y + 8 - d, 8)
        for h in range(2):
            held = full.at[h, lax.rem(x + 2, 4), core, from_y]
            arrive(held, xs.at[d, 2 + h], xr.at[d, 2 + h], mate)
            sent.append(push(held, held, cs.at[d, 3 + h], cr.at[d, 3 + h], mate))

    for step in range(12):
        if step < 8:
            near(order[step])
        if 2 <= step < 10:
            far(order[step - 2])
        if step >= 4:
            opposite(order[step - 4])
    for d in order:
        from_y = lax.rem(y + 8 - d, 8)
        for e, source in ((0, x), (1, lax.rem(x + 3, 4)), (2, lax.rem(x + 1, 4))):
            held = full.at[:, source, 1 - core, from_y]
            arrive(held, cs.at[d, e], cr.at[d, e], mate)
        for h in range(2):
            held = full.at[h, lax.rem(x + 2, 4), 1 - core, from_y]
            arrive(held, cs.at[d, 3 + h], cr.at[d, 3 + h], mate)
    for copy in sent:
        copy.wait_send()


def tile_kernel(visits, marg, table, counts, own_out, mate_out, log_marg, base, total):
    k = pl.program_id(0)
    own = lax.rem(lax.axis_index("row"), 16)
    core = lax.rem(lax.axis_index("col"), 2)

    @pl.when(k == 0)
    def _():
        log_marg[...] = jnp.log(marg[...].astype(F32))
        all_marg = marg[...]
        summed = jnp.sum(jnp.sum(all_marg, axis=0), axis=1, keepdims=True)
        log_total = jnp.log(summed.astype(F32))
        rows = jnp.broadcast_to(log_marg[own], (256, 256))
        base[...] = log_total - rows.T
        total[...] = jnp.zeros_like(total)

    row_vectors = table[own]
    terms = []
    row_term = None
    for i in range(STEP):
        visit = visits[k * STEP + i]
        col_vectors = table[visit]
        logits = lax.dot_general(
            row_vectors, col_vectors, (((1,), (1,)), ((), ())), preferred_element_type=F32
        )
        n = counts[i].astype(F32)
        margin = logits - (base[...] - log_marg[visit])
        m = jnp.maximum(n, 1.0)
        fitted = (0.1 + 0.25 * (m * lax.rsqrt(m))) * (margin - jnp.log(m))
        hinge = 0.5 * jnp.tanh(0.5 * margin) + 0.5
        g = (jnp.where(n > 0, fitted, hinge) * 0.0625).astype(BF16)
        term = jnp.dot(g, col_vectors, preferred_element_type=F32)
        row_term = term if row_term is None else row_term + term
        col_term = lax.dot_general(
            g, row_vectors, (((0,), (0,)), ((), ())), preferred_element_type=F32
        )
        terms.append((visit, col_term))
    total[own] += row_term
    for visit, col_term in terms:
        total[visit] += col_term

    @pl.when(k == K // STEP - 1)
    def _():
        for j in range(8):
            own_out[j] = total[2 * j + core]
            mate_out[j] = total[2 * j + 1 - core].astype(BF16)


def reduce_kernel(
    own_hbm, mate_part, out, own, own_sem, cbuf, xout, xin, kept, held, yout, yin, zout, zin,
    cs, cr, xs, xr, ys, yr, zs, zr, gs, gr,
):
    y, zl, zh, x, core = place()
    z = zh * 4 + zl
    fetch = pltpu.make_async_copy(own_hbm, own, own_sem)
    fetch.start()
    greet(partners(y, zl, zh, x, core))
    mate = device(y, zl, zh, x, 1 - core)
    right_x, left_x, far_x = lax.rem(x + 1, 4), lax.rem(x + 3, 4), lax.rem(x + 2, 4)
    right = device(y, zl, zh, right_x, core)
    left = device(y, zl, zh, left_x, core)
    sent = []
    order = (4, 3, 5, 2, 6, 1, 7, 0)
    for d in order:
        q = lax.rem(y + d, 8)
        sent.append(push(mate_part.at[:, :, q], cbuf.at[:, :, q], cs.at[d], cr.at[d], mate))

    fetch.wait()

    def send_x(d, slot, value, target):
        xout[d, slot] = value.astype(BF16)
        sent.append(push(xout.at[d, slot], xin.at[d, slot], xs.at[d, slot], xr.at[d, slot], target))

    def wait_x(d, slot):
        arrive(xin.at[d, slot], xs.at[d, slot], xr.at[d, slot], mate)
        return xin[d, slot].astype(F32)

    def first(d):
        q = lax.rem(y + d, 8)
        arrive(cbuf.at[:, :, q], cs.at[d], cr.at[d], mate)

        def chip(h, block):
            return own[h, block, q] + cbuf[h, block, q].astype(F32)

        send_x(d, 0, chip(0, far_x), right)
        send_x(d, 1, chip(1, far_x), left)
        send_x(d, 2, chip(1, right_x), right)
        send_x(d, 3, chip(0, left_x), left)
        kept[d, 0] = chip(0, right_x)
        kept[d, 1] = chip(1, left_x)
        held[d, 0] = chip(0, x)
        held[d, 1] = chip(1, x)

    def second(d):
        send_x(d, 4, kept[d, 0] + wait_x(d, 0), right)
        send_x(d, 5, kept[d, 1] + wait_x(d, 1), left)

    def third(d):
        low = held[d, 0] + wait_x(d, 3) + wait_x(d, 4)
        high = held[d, 1] + wait_x(d, 2) + wait_x(d, 5)
        if d:
            yout[d, 0] = low.astype(BF16)
            yout[d, 1] = high.astype(BF16)
            target = device(lax.rem(y + d, 8), zl, zh, x, core)
            sent.append(push(yout.at[d], yin.at[d], ys.at[d], yr.at[d], target))
        else:
            held[d, 0] = low
            held[d, 1] = high

    for step in range(12):
        if step < 8:
            first(order[step])
        if 2 <= step < 10:
            second(order[step - 2])
        if step >= 4:
            third(order[step - 4])
    summed = held[0]
    for d in (4, 3, 5, 2, 6, 1, 7):
        arrive(yin.at[d], ys.at[d], yr.at[d], mate)
        summed = summed + yin[d].astype(F32)
    zout[...] = summed.astype(BF16)
    for d in (4, 3, 5, 2, 6, 1, 7):
        other = lax.rem(z + d, 8)
        other_h = lax.div(other, 4)
        target = device(y, lax.rem(other, 4), other_h, x, core)
        sent.append(push(zout.at[other_h], zin.at[z], zs.at[d], zr.at[d], target))
    zin[z] = zout[zh]
    for d in (1, 7, 2, 6, 3, 5, 4):
        arrive(zin.at[lax.rem(z + 8 - d, 8)], zs.at[d], zr.at[d], mate)
    last = zin[0].astype(F32)
    for source in range(1, 8):
        last = last + zin[source].astype(F32)
    out[y] = last.astype(BF16)
    mine = out.at[y]
    for d in (4, 3, 5, 2, 6, 1, 7):
        target = device(lax.rem(y + d, 8), zl, zh, x, core)
        sent.append(push(mine, mine, gs.at[d], gr.at[d], target))
    for d in (1, 7, 2, 6, 3, 5, 4):
        arrive(out.at[lax.rem(y + 8 - d, 8)], gs.at[d], gr.at[d], mate)
    for copy in sent:
        copy.wait_send()


def whole():
    return pl.BlockSpec(memory_space=VMEM)


def local(table, marginals, visits, counts):
    sem = pltpu.SemaphoreType.DMA
    params = pltpu.CompilerParams
    full = pl.pallas_call(
        gather_kernel,
        out_shape=jax.ShapeDtypeStruct((2, 4, 2, 8, 32, 256), BF16),
        in_specs=[whole()],
        out_specs=whole(),
        scratch_shapes=[VMEM((8, 8, 256), F32)]
        + [sem((8,))] * 2
        + [sem((2, 5))] * 2
        + [sem((8, 4))] * 2
        + [sem((8, 5))] * 2,
        compiler_params=params(collective_id=0, has_side_effects=True),
        name="table_gather",
    )(table[0])
    full = full.reshape(16, 256, 256)
    own, mate_part = pl.pallas_call(
        tile_kernel,
        out_shape=[
            jax.ShapeDtypeStruct((8, 256, 256), F32),
            jax.ShapeDtypeStruct((8, 256, 256), BF16),
        ],
        grid_spec=pltpu.PrefetchScalarGridSpec(
            num_scalar_prefetch=1,
            grid=(K // STEP,),
            in_specs=[whole(), whole(), pl.BlockSpec((STEP, 256, 256), lambda k, v: (k, 0, 0))],
            out_specs=[whole(), whole()],
            scratch_shapes=[
                VMEM((16, 1, 256), F32),
                VMEM((256, 256), F32),
                VMEM((16, 256, 256), F32),
            ],
        ),
        name="tiles",
    )(visits[0, 0], marginals.reshape(16, 1, 256), full, counts[0, 0])
    out = pl.pallas_call(
        reduce_kernel,
        out_shape=jax.ShapeDtypeStruct((8, 32, 256), BF16),
        in_specs=[pl.BlockSpec(memory_space=pl.ANY)] * 2,
        out_specs=whole(),
        scratch_shapes=[
            VMEM((2, 4, 8, 32, 256), F32),
            sem(()),
            VMEM((2, 4, 8, 32, 256), BF16),
            VMEM((8, 6, 32, 256), BF16),
            VMEM((8, 6, 32, 256), BF16),
            VMEM((8, 2, 32, 256), F32),
            VMEM((8, 2, 32, 256), F32),
            VMEM((8, 2, 32, 256), BF16),
            VMEM((8, 2, 32, 256), BF16),
            VMEM((2, 32, 256), BF16),
            VMEM((8, 32, 256), BF16),
            sem((8,)), sem((8,)),
            sem((8, 6)), sem((8, 6)),
            sem((8,)), sem((8,)),
            sem((8,)), sem((8,)),
            sem((8,)), sem((8,)),
        ],
        compiler_params=params(collective_id=1, has_side_effects=True),
        name="gradient_reduce",
    )(own.reshape(2, 4, 8, 32, 256), mate_part.reshape(2, 4, 8, 32, 256))
    return out.reshape(1, 256, 256).astype(F32)


def solution(mesh):
    return jax.shard_map(
        local,
        mesh=mesh,
        in_specs=(
            P("col", "row", None),
            P(),
            P("row", "col", None),
            P("row", "col", None, None, None),
        ),
        out_specs=P("col", None, None),
        check_vma=False,
    )
```

```python
import jax
import jax.numpy as jnp
from jax import lax
from jax.experimental import pallas as pl
from jax.experimental.pallas import tpu as pltpu
from jax.sharding import PartitionSpec as P

K = 16
STEP = 4
MESH = pl.DeviceIdType.MESH
VMEM = pltpu.VMEM
F32 = jnp.float32
BF16 = jnp.bfloat16


def place():
    row = lax.axis_index("row")
    col = lax.axis_index("col")
    y, zl = lax.div(row, 4), lax.rem(row, 4)
    zh, x, core = lax.div(col, 8), lax.rem(lax.div(col, 2), 4), lax.rem(col, 2)
    return y, zl, zh, x, core


def device(y, zl, zh, x, core):
    return (y * 4 + zl, zh * 8 + x * 2 + core)


def partners(y, zl, zh, x, core):
    z = zh * 4 + zl
    found = [device(y, zl, zh, x, 1 - core)]
    for d in range(1, 4):
        found.append(device(y, zl, zh, lax.rem(x + d, 4), core))
    for d in range(1, 8):
        found.append(device(lax.rem(y + d, 8), zl, zh, x, core))
    for d in range(1, 8):
        other = lax.rem(z + d, 8)
        found.append(device(y, lax.rem(other, 4), lax.div(other, 4), x, core))
    return found


def greet(others):
    barrier = pltpu.get_barrier_semaphore()
    for other in others:
        pl.semaphore_signal(barrier, inc=1, device_id=other, device_id_type=MESH)
    pl.semaphore_wait(barrier, len(others))


def push(src, dst, send_sem, recv_sem, target):
    copy = pltpu.make_async_remote_copy(
        src_ref=src,
        dst_ref=dst,
        send_sem=send_sem,
        recv_sem=recv_sem,
        device_id=target,
        device_id_type=MESH,
    )
    copy.start()
    return copy


def arrive(dst, send_sem, recv_sem, target):
    pltpu.make_async_remote_copy(
        src_ref=dst,
        dst_ref=dst,
        send_sem=send_sem,
        recv_sem=recv_sem,
        device_id=target,
        device_id_type=MESH,
    ).wait_recv()


def gather_kernel(piece, full, zbuf, zs, zr, ys, yr, xs, xr, cs, cr):
    y, zl, zh, x, core = place()
    z = zh * 4 + zl
    greet(partners(y, zl, zh, x, core))
    mate = device(y, zl, zh, x, 1 - core)
    sent = []
    for d in (4, 3, 5, 2, 6, 1, 7):
        other = lax.rem(z + d, 8)
        target = device(y, lax.rem(other, 4), lax.div(other, 4), x, core)
        sent.append(push(piece, zbuf.at[z], zs.at[d], zr.at[d], target))
    zbuf[z] = piece[...]
    for d in range(1, 8):
        arrive(zbuf.at[lax.rem(z + 8 - d, 8)], zs.at[d], zr.at[d], mate)
    for h in range(2):
        full[h, x, core, y] = zbuf[h * 4 : h * 4 + 4].reshape(32, 256).astype(BF16)
    mine = full.at[:, x, core, y]
    up = device(lax.rem(y + 1, 8), zl, zh, x, core)
    down = device(lax.rem(y + 7, 8), zl, zh, x, core)
    up_two = device(lax.rem(y + 2, 8), zl, zh, x, core)
    down_two = device(lax.rem(y + 6, 8), zl, zh, x, core)
    sent.append(push(mine, mine, ys.at[0, 2], yr.at[0, 2], up_two))
    sent.append(push(mine, mine, ys.at[1, 2], yr.at[1, 2], down_two))
    sent.append(push(mine, mine, ys.at[0, 1], yr.at[0, 1], up))
    sent.append(push(mine, mine, ys.at[1, 1], yr.at[1, 1], down))
    right = device(y, zl, zh, lax.rem(x + 1, 4), core)
    left = device(y, zl, zh, lax.rem(x + 3, 4), core)
    order = (0, 2, 6, 1, 7, 3, 5, 4)

    def near(d):
        from_y = lax.rem(y + 8 - d, 8)
        held = full.at[:, x, core, from_y]
        if d == 4:
            arrive(full.at[0, x, core, from_y], ys.at[0, 4], yr.at[0, 4], mate)
            arrive(full.at[1, x, core, from_y], ys.at[1, 4], yr.at[1, 4], mate)
        elif d:
            side, hops = (0, d) if d < 4 else (1, 8 - d)
            arrive(held, ys.at[side, hops], yr.at[side, hops], mate)
            if hops == 2:
                half = full.at[side, x, core, from_y]
                far_target = (up_two, down_two)[side]
                sent.append(push(half, half, ys.at[side, 4], yr.at[side, 4], far_target))
                next_target = (up, down)[side]
                sent.append(push(held, held, ys.at[side, 3], yr.at[side, 3], next_target))
        sent.append(push(held, held, xs.at[d, 0], xr.at[d, 0], right))
        sent.append(push(held, held, xs.at[d, 1], xr.at[d, 1], left))
        sent.append(push(held, held, cs.at[d, 0], cr.at[d, 0], mate))

    def far(d):
        from_y = lax.rem(y + 8 - d, 8)
        before = full.at[:, lax.rem(x + 3, 4), core, from_y]
        after = full.at[:, lax.rem(x + 1, 4), core, from_y]
        arrive(before, xs.at[d, 0], xr.at[d, 0], mate)
        half = full.at[0, lax.rem(x + 3, 4), core, from_y]
        sent.append(push(half, half, xs.at[d, 2], xr.at[d, 2], right))
        arrive(after, xs.at[d, 1], xr.at[d, 1], mate)
        half = full.at[1, lax.rem(x + 1, 4), core, from_y]
        sent.append(push(half, half, xs.at[d, 3], xr.at[d, 3], left))
        sent.append(push(before, before, cs.at[d, 1], cr.at[d, 1], mate))
        sent.append(push(after, after, cs.at[d, 2], cr.at[d, 2], mate))

    def opposite(d):
        from_y = lax.rem(y + 8 - d, 8)
        for h in range(2):
            held = full.at[h, lax.rem(x + 2, 4), core, from_y]
            arrive(held, xs.at[d, 2 + h], xr.at[d, 2 + h], mate)
            sent.append(push(held, held, cs.at[d, 3 + h], cr.at[d, 3 + h], mate))

    for step in range(17):
        if step < 8:
            near(order[step])
        if 5 <= step < 13:
            far(order[step - 5])
        if step >= 9:
            opposite(order[step - 9])
    for d in order:
        from_y = lax.rem(y + 8 - d, 8)
        for e, source in ((0, x), (1, lax.rem(x + 3, 4)), (2, lax.rem(x + 1, 4))):
            held = full.at[:, source, 1 - core, from_y]
            arrive(held, cs.at[d, e], cr.at[d, e], mate)
        for h in range(2):
            held = full.at[h, lax.rem(x + 2, 4), 1 - core, from_y]
            arrive(held, cs.at[d, 3 + h], cr.at[d, 3 + h], mate)
    for copy in sent:
        copy.wait_send()


def tile_kernel(visits, marg, table, counts, own_out, mate_out, log_marg, base, total):
    k = pl.program_id(0)
    own = lax.rem(lax.axis_index("row"), 16)
    core = lax.rem(lax.axis_index("col"), 2)

    @pl.when(k == 0)
    def _():
        log_marg[...] = jnp.log(marg[...].astype(F32))
        all_marg = marg[...]
        summed = jnp.sum(jnp.sum(all_marg, axis=0), axis=1, keepdims=True)
        log_total = jnp.log(summed.astype(F32))
        rows = jnp.broadcast_to(log_marg[own], (256, 256))
        base[...] = log_total - rows.T
        total[...] = jnp.zeros_like(total)

    row_vectors = table[own]
    terms = []
    row_term = None
    for i in range(STEP):
        visit = visits[k * STEP + i]
        col_vectors = table[visit]
        logits = lax.dot_general(
            row_vectors, col_vectors, (((1,), (1,)), ((), ())), preferred_element_type=F32
        )
        n = counts[i].astype(F32)
        margin = logits - (base[...] - log_marg[visit])
        m = jnp.maximum(n, 1.0)
        fitted = (0.1 + 0.25 * (m * lax.rsqrt(m))) * (margin - jnp.log(m))
        hinge = 0.5 * jnp.tanh(0.5 * margin) + 0.5
        g = (jnp.where(n > 0, fitted, hinge) * 0.0625).astype(BF16)
        term = jnp.dot(g, col_vectors, preferred_element_type=F32)
        row_term = term if row_term is None else row_term + term
        col_term = lax.dot_general(
            g, row_vectors, (((0,), (0,)), ((), ())), preferred_element_type=F32
        )
        terms.append((visit, col_term))
    total[own] += row_term
    for visit, col_term in terms:
        total[visit] += col_term

    @pl.when(k == K // STEP - 1)
    def _():
        for j in range(8):
            own_out[j] = total[2 * j + core]
            mate_out[j] = total[2 * j + 1 - core].astype(BF16)


def reduce_kernel(
    own_hbm, mate_part, out, own, own_sem, cbuf, xout, xin, kept, held, yout, yin, zout, zin,
    cs, cr, xs, xr, ys, yr, zs, zr, gs, gr,
):
    y, zl, zh, x, core = place()
    z = zh * 4 + zl
    fetch = pltpu.make_async_copy(own_hbm, own, own_sem)
    fetch.start()
    greet(partners(y, zl, zh, x, core))
    mate = device(y, zl, zh, x, 1 - core)
    right_x, left_x, far_x = lax.rem(x + 1, 4), lax.rem(x + 3, 4), lax.rem(x + 2, 4)
    right = device(y, zl, zh, right_x, core)
    left = device(y, zl, zh, left_x, core)
    sent = []
    order = (4, 3, 5, 2, 6, 1, 7, 0)
    for d in order:
        q = lax.rem(y + d, 8)
        sent.append(push(mate_part.at[:, :, q], cbuf.at[:, :, q], cs.at[d], cr.at[d], mate))

    fetch.wait()

    def send_x(d, slot, value, target):
        xout[d, slot] = value.astype(BF16)
        sent.append(push(xout.at[d, slot], xin.at[d, slot], xs.at[d, slot], xr.at[d, slot], target))

    def wait_x(d, slot):
        arrive(xin.at[d, slot], xs.at[d, slot], xr.at[d, slot], mate)
        return xin[d, slot].astype(F32)

    def first(d):
        q = lax.rem(y + d, 8)
        arrive(cbuf.at[:, :, q], cs.at[d], cr.at[d], mate)

        def chip(h, block):
            return own[h, block, q] + cbuf[h, block, q].astype(F32)

        send_x(d, 0, chip(0, far_x), right)
        send_x(d, 1, chip(1, far_x), left)
        send_x(d, 2, chip(1, right_x), right)
        send_x(d, 3, chip(0, left_x), left)
        kept[d, 0] = chip(0, right_x)
        kept[d, 1] = chip(1, left_x)
        held[d, 0] = chip(0, x)
        held[d, 1] = chip(1, x)

    def second(d):
        send_x(d, 4, kept[d, 0] + wait_x(d, 0), right)
        send_x(d, 5, kept[d, 1] + wait_x(d, 1), left)

    def third(d):
        low = held[d, 0] + wait_x(d, 3) + wait_x(d, 4)
        high = held[d, 1] + wait_x(d, 2) + wait_x(d, 5)
        if d:
            yout[d, 0] = low.astype(BF16)
            yout[d, 1] = high.astype(BF16)
            target = device(lax.rem(y + d, 8), zl, zh, x, core)
            sent.append(push(yout.at[d], yin.at[d], ys.at[d], yr.at[d], target))
        else:
            held[d, 0] = low
            held[d, 1] = high

    for step in range(12):
        if step < 8:
            first(order[step])
        if 2 <= step < 10:
            second(order[step - 2])
        if step >= 4:
            third(order[step - 4])
    summed = held[0]
    for d in (4, 3, 5, 2, 6, 1, 7):
        arrive(yin.at[d], ys.at[d], yr.at[d], mate)
        summed = summed + yin[d].astype(F32)
    zout[...] = summed.astype(BF16)
    for d in (4, 3, 5, 2, 6, 1, 7):
        other = lax.rem(z + d, 8)
        other_h = lax.div(other, 4)
        target = device(y, lax.rem(other, 4), other_h, x, core)
        sent.append(push(zout.at[other_h], zin.at[z], zs.at[d], zr.at[d], target))
    zin[z] = zout[zh]
    for d in (1, 7, 2, 6, 3, 5, 4):
        arrive(zin.at[lax.rem(z + 8 - d, 8)], zs.at[d], zr.at[d], mate)
    last = zin[0].astype(F32)
    for source in range(1, 8):
        last = last + zin[source].astype(F32)
    out[y] = last.astype(BF16)
    mine = out.at[y]
    for d in (4, 3, 5, 2, 6, 1, 7):
        target = device(lax.rem(y + d, 8), zl, zh, x, core)
        sent.append(push(mine, mine, gs.at[d], gr.at[d], target))
    for d in (1, 7, 2, 6, 3, 5, 4):
        arrive(out.at[lax.rem(y + 8 - d, 8)], gs.at[d], gr.at[d], mate)
    for copy in sent:
        copy.wait_send()


def whole():
    return pl.BlockSpec(memory_space=VMEM)


def local(table, marginals, visits, counts):
    sem = pltpu.SemaphoreType.DMA
    params = pltpu.CompilerParams
    full = pl.pallas_call(
        gather_kernel,
        out_shape=jax.ShapeDtypeStruct((2, 4, 2, 8, 32, 256), BF16),
        in_specs=[whole()],
        out_specs=whole(),
        scratch_shapes=[VMEM((8, 8, 256), F32)]
        + [sem((8,))] * 2
        + [sem((2, 5))] * 2
        + [sem((8, 4))] * 2
        + [sem((8, 5))] * 2,
        compiler_params=params(collective_id=0, has_side_effects=True),
        name="table_gather",
    )(table[0])
    full = full.reshape(16, 256, 256)
    own, mate_part = pl.pallas_call(
        tile_kernel,
        out_shape=[
            jax.ShapeDtypeStruct((8, 256, 256), F32),
            jax.ShapeDtypeStruct((8, 256, 256), BF16),
        ],
        grid_spec=pltpu.PrefetchScalarGridSpec(
            num_scalar_prefetch=1,
            grid=(K // STEP,),
            in_specs=[whole(), whole(), pl.BlockSpec((STEP, 256, 256), lambda k, v: (k, 0, 0))],
            out_specs=[whole(), whole()],
            scratch_shapes=[
                VMEM((16, 1, 256), F32),
                VMEM((256, 256), F32),
                VMEM((16, 256, 256), F32),
            ],
        ),
        name="tiles",
    )(visits[0, 0], marginals.reshape(16, 1, 256), full, counts[0, 0])
    out = pl.pallas_call(
        reduce_kernel,
        out_shape=jax.ShapeDtypeStruct((8, 32, 256), BF16),
        in_specs=[pl.BlockSpec(memory_space=pl.ANY)] * 2,
        out_specs=whole(),
        scratch_shapes=[
            VMEM((2, 4, 8, 32, 256), F32),
            sem(()),
            VMEM((2, 4, 8, 32, 256), BF16),
            VMEM((8, 6, 32, 256), BF16),
            VMEM((8, 6, 32, 256), BF16),
            VMEM((8, 2, 32, 256), F32),
            VMEM((8, 2, 32, 256), F32),
            VMEM((8, 2, 32, 256), BF16),
            VMEM((8, 2, 32, 256), BF16),
            VMEM((2, 32, 256), BF16),
            VMEM((8, 32, 256), BF16),
            sem((8,)), sem((8,)),
            sem((8, 6)), sem((8, 6)),
            sem((8,)), sem((8,)),
            sem((8,)), sem((8,)),
            sem((8,)), sem((8,)),
        ],
        compiler_params=params(collective_id=1, has_side_effects=True),
        name="gradient_reduce",
    )(own.reshape(2, 4, 8, 32, 256), mate_part.reshape(2, 4, 8, 32, 256))
    return out.reshape(1, 256, 256).astype(F32)


def solution(mesh):
    return jax.shard_map(
        local,
        mesh=mesh,
        in_specs=(
            P("col", "row", None),
            P(),
            P("row", "col", None),
            P("row", "col", None, None, None),
        ),
        out_specs=P("col", None, None),
        check_vma=False,
    )
```
